32 devices in a mesh: dp: 8 (over y, x, core), tensor: 4 (over z).
Axes of the slice: x: 2, y: 2, z: 4, core: 2. Of those that a mesh axis runs over, the one named last changes fastest.
Arguments:
- hidden_in: float32 [8192, 1536], P(('dp', 'tensor')), may hold values from -6 to 6
- cotangent: float32 [8192, 1536], P(('dp', 'tensor')), may hold values from -6 to 6
- seq_lengths: int32 [8, 4], P('dp'), may hold values from 1 to 512, 1024 in all within a row
- query_weight: bfloat16 [1536, 1536], P('dp', 'tensor'), may hold values from -0.15625 to 0.15625
- key_weight: bfloat16 [1536, 768], P('dp', 'tensor'), may hold values from -0.15625 to 0.15625
- value_weight: bfloat16 [1536, 768], P('dp', 'tensor'), may hold values from -0.15625 to 0.15625
- output_weight: bfloat16 [1536, 1536], P('tensor', 'dp'), may hold values from -1.25 to 1.25
- w_gate: bfloat16 [1536, 4096], P('dp', 'tensor'), may hold values from -0.15625 to 0.15625
- w_up: bfloat16 [1536, 4096], P('dp', 'tensor'), may hold values from -0.15625 to 0.15625
- w_down: bfloat16 [4096, 1536], P('tensor', 'dp'), may hold values from -0.09375 to 0.09375
- gain_attn: bfloat16 [1536], P('dp'), may hold values from 0.099609375 to 1.8984375
- gain_mlp: bfloat16 [1536], P('dp'), may hold values from 0.099609375 to 1.8984375
Outputs:
- block_out: float32 [8192, 1536], P(('dp', 'tensor'))
- grad_input: float32 [8192, 1536], P(('dp', 'tensor'))
- grad_query: float32 [1536, 1536], P('dp', 'tensor')
- grad_key: float32 [1536, 768], P('dp', 'tensor')
- grad_value: float32 [1536, 768], P('dp', 'tensor')
- grad_output: float32 [1536, 1536], P('tensor', 'dp')
- grad_gate: float32 [1536, 4096], P('dp', 'tensor')
- grad_upproj: float32 [1536, 4096], P('dp', 'tensor')
- grad_down: float32 [4096, 1536], P('tensor', 'dp')
- grad_attnorm: float32 [1536], P('dp')
- grad_mlpnorm: float32 [1536], P('dp')
The draws below stay inside these ranges and needn't reach their ends.
Inputs may be any that keep to these rules, and one draw needn't show every extreme that they name: `seq_lengths`: each row's lengths sum to 1024, and the longest of each row is exactly 512.
All inputs are finite; a program needn't handle non-finite values.
Results may differ from the reference program's by a relative error of at most 0.02.
Values may be sent and summed in bfloat16 or wider, within the bound.
No kernel may reach another device: no remote copies, remote signals or barrier semaphores. Data moves between devices by JAX's collectives and lax.ppermute only.
A program may use at most 128 MiB of HBM per device.

```python
import math
import jax
import jax.numpy as jnp
import numpy as np
from jax import lax

MODEL_WIDTH = 1536
QUERY_HEADS = 16
KEY_VALUE_HEADS = 8
HEAD_SIZE = 96
FF = 4096
TOKENS_PER_SHARD = 1024
NSEQ = 4
MOSTLEN = 512
TOKENS = 8192
N_DP = 8


def raised(drawn, own_key, source, target, shards_of, factor):
    owner, partner = [(jnp.arange(drawn.shape[axis_at]) // (drawn.shape[axis_at] // shards_of)).reshape([-1 if axis == axis_at else 1 for axis in range(drawn.ndim)]) for axis_at in (source, target)]
    chosen = jax.random.permutation(own_key, shards_of)[partner]
    strong = (owner == chosen) | (owner == (partner + shards_of // 2) % shards_of)
    return jnp.where(strong, factor * drawn, drawn)


def level_of(own_key, shape, cuts, smallest, top_value):
    loudness, own = 1.0, jax.random.fold_in(own_key, 6)
    for dim, blocks in cuts:
        steps = jnp.exp(jax.random.uniform(jax.random.fold_in(own, dim), (blocks,), jnp.float32, smallest / len(cuts), top_value / len(cuts)))
        loudness = loudness * jnp.repeat(steps, shape[dim] // blocks).reshape([-1 if axis == dim else 1 for axis in range(len(shape))])
    return loudness


def profile(count, total, limit, slope):
    weights = [(1 << 20) // math.isqrt(standing ** slope) + 1 for standing in range(2, count + 1)]
    rest, counts = total - limit - (count - 1), [1] * (count - 1)
    while rest > 0:
        candidates = [i for i in range(count - 1) if counts[i] < limit]
        mass, remaining = sum([weights[i] for i in candidates]), rest
        for i in candidates:
            addition = min(limit - counts[i], max(1, remaining * weights[i] // mass), rest)
            counts[i] = counts[i] + addition
            rest = rest - addition
    return np.array([limit] + counts)


def ragged_sizes(key, number_of, total, most, skew):
    if number_of == 2:
        one = jax.random.randint(key, (), max(1, total - most), min(most, total - 1) + 1)
        return jnp.stack([one, total - one])
    sizes = jnp.asarray(profile(number_of, total, most, skew), jnp.int32)
    twos = (number_of - 1) // 2
    source_of, sink = sizes[1:1 + 2 * twos:2], sizes[2:2 + 2 * twos:2]
    margin = jnp.minimum(source_of - 1, most - sink)
    shifted = jax.random.randint(jax.random.fold_in(key, 1), (twos,), 0, 1 << 20) % (margin + 1)
    sizes = sizes.at[1:1 + 2 * twos:2].set(source_of - shifted).at[2:2 + 2 * twos:2].set(sink + shifted)
    return sizes[jax.random.permutation(jax.random.fold_in(key, 2), number_of)]


def normal_values(rng, shape, spread, bound, cuts=(), kind=jnp.bfloat16):
    values = jax.random.normal(rng, shape, jnp.float32) * spread
    if len(cuts) > 0:
        values = level_of(rng, shape, cuts, -0.22, 0.18) * values
    return jnp.clip(values, min=-bound, max=bound).astype(kind)


def heavy_noise(stream_key, shape, scale, reach, cuts, heavy, kind=jnp.bfloat16):
    entries = scale * jax.random.normal(stream_key, shape, jnp.float32)
    if cuts:
        entries = entries * level_of(stream_key, shape, cuts, -0.22, 0.18)
    return jnp.clip(raised(entries, jax.random.fold_in(stream_key, 3), *heavy), -reach, reach).astype(kind)


def setup_inputs(seed: int = 0) -> dict:
    arg_keys = jax.random.split(jax.random.key(seed), 13)
    hidden_in = normal_values(arg_keys[0], (TOKENS, MODEL_WIDTH), 1.0, 6.0, ((0, 32),), jnp.float32)
    cotangent = heavy_noise(arg_keys[1], (TOKENS, MODEL_WIDTH), 1.0, 6.0, ((0, 32),), (0, 1, 32, 2.75), jnp.float32)
    seq_lengths = jax.vmap(lambda own: ragged_sizes(own, NSEQ, TOKENS_PER_SHARD, MOSTLEN, 2))(jax.random.split(arg_keys[2], N_DP)).reshape((N_DP, NSEQ)).astype(jnp.int32)
    query_weight = normal_values(arg_keys[3], (MODEL_WIDTH, QUERY_HEADS * HEAD_SIZE), MODEL_WIDTH ** -0.5, 0.15625, ((0, 8), (1, 4)))
    key_weight = normal_values(arg_keys[4], (MODEL_WIDTH, KEY_VALUE_HEADS * HEAD_SIZE), MODEL_WIDTH ** -0.5, 0.15625, ((0, 8), (1, 4)))
    value_weight = normal_values(arg_keys[5], (MODEL_WIDTH, KEY_VALUE_HEADS * HEAD_SIZE), MODEL_WIDTH ** -0.5, 0.15625, ((0, 8), (1, 4)))
    output_weight = normal_values(arg_keys[6], (QUERY_HEADS * HEAD_SIZE, MODEL_WIDTH), (QUERY_HEADS * HEAD_SIZE // 64) ** -0.5, 1.25, ((0, 4), (1, 8)))
    w_gate = normal_values(arg_keys[7], (MODEL_WIDTH, FF), MODEL_WIDTH ** -0.5, 0.15625, ((0, 8), (1, 4)))
    w_up = normal_values(arg_keys[8], (MODEL_WIDTH, FF), MODEL_WIDTH ** -0.5, 0.15625, ((0, 8), (1, 4)))
    w_down = normal_values(arg_keys[9], (FF, MODEL_WIDTH), FF ** -0.5, 0.09375, ((0, 4), (1, 8)))
    gain_attn = jnp.clip(1.0 + 0.18 * jax.random.normal(arg_keys[10], (MODEL_WIDTH,), jnp.float32), 0.099609375, 1.8984375).astype(jnp.bfloat16)
    gain_mlp = jnp.clip(1.0 + 0.18 * jax.random.normal(arg_keys[11], (MODEL_WIDTH,), jnp.float32), 0.099609375, 1.8984375).astype(jnp.bfloat16)
    return dict(hidden_in=hidden_in, cotangent=cotangent, seq_lengths=seq_lengths, query_weight=query_weight, key_weight=key_weight, value_weight=value_weight, output_weight=output_weight, w_gate=w_gate, w_up=w_up, w_down=w_down, gain_attn=gain_attn, gain_mlp=gain_mlp)


EPS = 1e-05
ROPE_BASE = 100000.0

def product(formula, left_side, right_side):
    return jnp.einsum(formula, left_side.astype(jnp.float32), right_side.astype(jnp.float32), precision=lax.Precision.HIGHEST)

def matrix_multiply(left_side, right_side):
    return jnp.dot(left_side, right_side, preferred_element_type=jnp.float32)

def multiply_by_transpose(left_side, right_side):
    return lax.dot_general(left_side, right_side, (((1,), (1,)), ((), ())), preferred_element_type=jnp.float32)

def transposed_times(left_side, right_side):
    return lax.dot_general(left_side, right_side, (((0,), (0,)), ((), ())), preferred_element_type=jnp.float32)

def positions_of(lengths_row, length_all):
    seq_ends = jnp.cumsum(lengths_row).astype(jnp.int32)
    seq_starts = seq_ends - lengths_row
    token_index = jnp.arange(length_all, dtype=jnp.int32)
    segment = lax.optimization_barrier(jnp.sum((token_index[:, None] >= seq_ends[None, :]).astype(jnp.int32), axis=1))
    chosen = segment[:, None] == jnp.arange(lengths_row.shape[0], dtype=jnp.int32)[None, :]
    offsets = lax.optimization_barrier(jnp.sum(jnp.where(chosen, seq_starts[None, :], 0), axis=1))
    return (segment, token_index - offsets)

def rope_tables(position, head_width):
    half_width = head_width // 2
    frequency = jnp.exp(-(2.0 * jnp.arange(half_width, dtype=jnp.float32) / head_width) * jnp.log(jnp.float32(ROPE_BASE)))
    angles = position.astype(jnp.float32)[:, None] * frequency[None, :]
    return (jnp.cos(angles), jnp.sin(angles))

def rotate_fwd(value_tensor, cosine, sine):
    half_width = value_tensor.shape[-1] // 2
    front_half = value_tensor[..., :half_width]
    back_half = value_tensor[..., half_width:]
    return jnp.concatenate([front_half * cosine - back_half * sine, back_half * cosine + front_half * sine], axis=-1)

def inverse_rotation(value_tensor, cosine, sine):
    half_width = value_tensor.shape[-1] // 2
    front_half = value_tensor[..., :half_width]
    back_half = value_tensor[..., half_width:]
    return jnp.concatenate([front_half * cosine + back_half * sine, back_half * cosine - front_half * sine], axis=-1)

def norm_forward(value_tensor, gain_vector):
    inverse = lax.rsqrt(lax.optimization_barrier(jnp.mean(value_tensor * value_tensor, axis=-1, keepdims=True)) + EPS)
    unit_rows = value_tensor * inverse
    return (unit_rows, inverse, (unit_rows * gain_vector.astype(jnp.float32)).astype(jnp.bfloat16))

def norm_backward(grad_normed, unit_rows, inverse, gain_vector):
    scaled = grad_normed * gain_vector.astype(jnp.float32)
    grad_gain = lax.optimization_barrier(jnp.sum(grad_normed * unit_rows, axis=0))
    grad_rows = inverse * (scaled - unit_rows * lax.optimization_barrier(jnp.mean(scaled * unit_rows, axis=-1, keepdims=True)))
    return (grad_rows, grad_gain)

def block_scores(query_block, key_rows, segment_block, index_block, segment, factor):
    scores = product('qkgd,skd->kgqs', query_block, key_rows) * factor
    length_all = key_rows.shape[0]
    allowed = (segment_block[:, None] == segment[None, :]) & (jnp.arange(length_all, dtype=jnp.int32)[None, :] <= index_block[:, None])
    return jnp.where(allowed[None, None], scores, -jnp.inf)

def attend(queries, key_rows, value_row_block, segment, block_rows):
    length_all, kv_heads, query_group_width, head_width = queries.shape
    blocks = length_all // block_rows
    factor = 1.0 / math.sqrt(head_width)
    token_index = jnp.arange(length_all, dtype=jnp.int32)

    def per_block(pieces):
        query_block, segment_block, index_block = pieces
        scores = block_scores(query_block, key_rows, segment_block, index_block, segment, factor)
        maximum = lax.optimization_barrier(jnp.max(scores, axis=-1, keepdims=True))
        logsum = maximum + jnp.log(lax.optimization_barrier(jnp.sum(jnp.exp(scores - maximum), axis=-1, keepdims=True)))
        weights = jnp.exp(scores - logsum).astype(jnp.bfloat16)
        mixed = product('kgqs,skd->qkgd', weights, value_row_block).astype(jnp.bfloat16)
        return (mixed, logsum[..., 0])
    mixed, logsum = lax.map(per_block, (queries.reshape(blocks, block_rows, kv_heads, query_group_width, head_width), segment.reshape(blocks, block_rows), token_index.reshape(blocks, block_rows)))
    return (mixed.reshape(length_all, kv_heads, query_group_width, head_width), logsum)

def attend_back(queries, key_rows, value_row_block, mixed, mixed_gradient, logsum, segment, block_rows):
    length_all, kv_heads, query_group_width, head_width = queries.shape
    blocks = length_all // block_rows
    factor = 1.0 / math.sqrt(head_width)
    token_index = jnp.arange(length_all, dtype=jnp.int32)

    def per_block(carry, pieces):
        grad_keys, grad_values = carry
        query_block, mixed_block, grad_block, logsum_block, segment_block, index_block = pieces
        scores = block_scores(query_block, key_rows, segment_block, index_block, segment, factor)
        probability = jnp.exp(scores - logsum_block[..., None])
        grad_values = grad_values + product('kgqs,qkgd->skd', probability.astype(jnp.bfloat16), grad_block)
        grad_probs = product('qkgd,skd->kgqs', grad_block, value_row_block)
        row_delta = lax.optimization_barrier(jnp.sum(grad_block.astype(jnp.float32) * mixed_block.astype(jnp.float32), axis=-1))
        row_delta = jnp.transpose(row_delta, (1, 2, 0))[..., None]
        grad_scores = (probability * (grad_probs - row_delta) * factor).astype(jnp.bfloat16)
        grad_query = product('kgqs,skd->qkgd', grad_scores, key_rows)
        grad_keys = grad_keys + product('kgqs,qkgd->skd', grad_scores, query_block)
        return ((grad_keys, grad_values), grad_query)
    empty_grad = jnp.zeros((length_all, kv_heads, head_width), jnp.float32)
    shape_blocks = (blocks, block_rows, kv_heads, query_group_width, head_width)
    (grad_keys, grad_values), grad_query = lax.scan(per_block, (empty_grad, empty_grad), (queries.reshape(shape_blocks), mixed.reshape(shape_blocks), mixed_gradient.reshape(shape_blocks), logsum, segment.reshape(blocks, block_rows), token_index.reshape(blocks, block_rows)))
    return (grad_query.reshape(length_all, kv_heads, query_group_width, head_width), grad_keys, grad_values)

def reference(hidden_in, cotangent, seq_lengths, query_weight, key_weight, value_weight, output_weight, w_gate, w_up, w_down, gain_attn, gain_mlp):
    query_group_width = QUERY_HEADS // KEY_VALUE_HEADS
    block_rows = min(512, TOKENS_PER_SHARD)

    def per_dp_block(carry, pieces):
        block_in, block_cot, lengths_row = pieces
        unit_one, inverse_one, first_normalized = norm_forward(block_in, gain_attn)
        segment, position = positions_of(lengths_row, TOKENS_PER_SHARD)
        cosine, sine = rope_tables(position, HEAD_SIZE)
        cos_heads, sin_heads = (cosine[:, None, None, :], sine[:, None, None, :])
        cosine_key_table, sine_key_table = (cosine[:, None, :], sine[:, None, :])
        unrotated_queries = matrix_multiply(first_normalized, query_weight).reshape(TOKENS_PER_SHARD, KEY_VALUE_HEADS, query_group_width, HEAD_SIZE)
        unrotated_keys = matrix_multiply(first_normalized, key_weight).reshape(TOKENS_PER_SHARD, KEY_VALUE_HEADS, HEAD_SIZE)
        value_row_block = matrix_multiply(first_normalized, value_weight).astype(jnp.bfloat16).reshape(TOKENS_PER_SHARD, KEY_VALUE_HEADS, HEAD_SIZE)
        query_rot = rotate_fwd(unrotated_queries, cos_heads, sin_heads).astype(jnp.bfloat16)
        key_rot = rotate_fwd(unrotated_keys, cosine_key_table, sine_key_table).astype(jnp.bfloat16)
        mixed, logsum = attend(query_rot, key_rot, value_row_block, segment, block_rows)
        mixed_flat = mixed.reshape(TOKENS_PER_SHARD, QUERY_HEADS * HEAD_SIZE)
        residual = block_in + matrix_multiply(mixed_flat, output_weight)
        unit_two, inverse_two, normed_two = norm_forward(residual, gain_mlp)
        gate_rows = matrix_multiply(normed_two, w_gate)
        up_rows = matrix_multiply(normed_two, w_up)
        sigmoid_gate = jax.nn.sigmoid(gate_rows)
        silu_gate = gate_rows * sigmoid_gate
        hidden_act = (silu_gate * up_rows).astype(jnp.bfloat16)
        block_out = residual + matrix_multiply(hidden_act, w_down)
        cot_low = block_cot.astype(jnp.bfloat16)
        grad_act = multiply_by_transpose(cot_low, w_down)
        grad_down = transposed_times(hidden_act, cot_low)
        grad_gate_rows = (grad_act * up_rows * sigmoid_gate * (1.0 + gate_rows * (1.0 - sigmoid_gate))).astype(jnp.bfloat16)
        grad_up_rows = (grad_act * silu_gate).astype(jnp.bfloat16)
        grad_gate = transposed_times(normed_two, grad_gate_rows)
        grad_upproj = transposed_times(normed_two, grad_up_rows)
        grad_normed_two = multiply_by_transpose(grad_gate_rows, w_gate) + multiply_by_transpose(grad_up_rows, w_up)
        grad_middle, grad_gain_two = norm_backward(grad_normed_two, unit_two, inverse_two, gain_mlp)
        grad_resid = block_cot + grad_middle
        narrow_gradient = grad_resid.astype(jnp.bfloat16)
        grad_output = transposed_times(mixed_flat, narrow_gradient)
        mixed_gradient = multiply_by_transpose(narrow_gradient, output_weight).astype(jnp.bfloat16).reshape(TOKENS_PER_SHARD, KEY_VALUE_HEADS, query_group_width, HEAD_SIZE)
        grad_qrot, rotated_key_gradient, gradient_values_list = attend_back(query_rot, key_rot, value_row_block, mixed, mixed_gradient, logsum, segment, block_rows)
        grad_q = inverse_rotation(grad_qrot, cos_heads, sin_heads).astype(jnp.bfloat16).reshape(TOKENS_PER_SHARD, QUERY_HEADS * HEAD_SIZE)
        key_gradient = inverse_rotation(rotated_key_gradient, cosine_key_table, sine_key_table).astype(jnp.bfloat16).reshape(TOKENS_PER_SHARD, KEY_VALUE_HEADS * HEAD_SIZE)
        value_gradient = gradient_values_list.astype(jnp.bfloat16).reshape(TOKENS_PER_SHARD, KEY_VALUE_HEADS * HEAD_SIZE)
        grad_query = transposed_times(first_normalized, grad_q)
        grad_key = transposed_times(first_normalized, key_gradient)
        grad_value = transposed_times(first_normalized, value_gradient)
        grad_normed_one = multiply_by_transpose(grad_q, query_weight) + multiply_by_transpose(key_gradient, key_weight) + multiply_by_transpose(value_gradient, value_weight)
        grad_first, grad_gain_one = norm_backward(grad_normed_one, unit_one, inverse_one, gain_attn)
        grad_in = grad_resid + grad_first
        updates = (grad_query, grad_key, grad_value, grad_output, grad_gate, grad_upproj, grad_down, grad_gain_one, grad_gain_two)
        carry = tuple((total + update for total, update in zip(carry, updates)))
        return (carry, (block_out, grad_in))
    start_carry = tuple((jnp.zeros(weight.shape, jnp.float32) for weight in (query_weight, key_weight, value_weight, output_weight, w_gate, w_up, w_down, gain_attn, gain_mlp)))
    carry, (outputs, grads) = lax.scan(per_dp_block, start_carry, (hidden_in.reshape(N_DP, TOKENS_PER_SHARD, MODEL_WIDTH), cotangent.reshape(N_DP, TOKENS_PER_SHARD, MODEL_WIDTH), seq_lengths))
    return (outputs.reshape(TOKENS, MODEL_WIDTH), grads.reshape(TOKENS, MODEL_WIDTH), carry[0], carry[1], carry[2], carry[3], carry[4], carry[5], carry[6], carry[7], carry[8])
```

```python
import math

import jax
import jax.numpy as jnp
from jax import lax
from jax.experimental import pallas as pl
from jax.experimental.pallas import tpu as pltpu
from jax.sharding import PartitionSpec as P

QUERY_HEADS = 16
KEY_VALUE_HEADS = 8
HEAD_SIZE = 96


EPS = 1e-05
ROPE_BASE = 100000.0


def product(formula, left_side, right_side):
    return jnp.einsum(formula, left_side, right_side, preferred_element_type=jnp.float32)


def matrix_multiply(left_side, right_side):
    return jnp.dot(left_side, right_side, preferred_element_type=jnp.float32)


def multiply_by_transpose(left_side, right_side):
    return lax.dot_general(
        left_side, right_side, (((1,), (1,)), ((), ())), preferred_element_type=jnp.float32
    )


def transposed_times(left_side, right_side):
    return lax.dot_general(
        left_side, right_side, (((0,), (0,)), ((), ())), preferred_element_type=jnp.float32
    )


def positions_of(lengths_row, length_all):
    seq_ends = jnp.cumsum(lengths_row)
    seq_starts = seq_ends - lengths_row
    token_index = jnp.arange(length_all, dtype=jnp.int32)
    segment = jnp.sum((token_index[:, None] >= seq_ends[None, :]).astype(jnp.int32), axis=1)
    chosen = segment[:, None] == jnp.arange(lengths_row.shape[0], dtype=jnp.int32)[None, :]
    offsets = jnp.sum(jnp.where(chosen, seq_starts[None, :], 0), axis=1)
    return (segment, token_index - offsets)


def rope_tables(position, head_width):
    half_width = head_width // 2
    frequency = jnp.exp(
        -(2.0 * jnp.arange(half_width, dtype=jnp.float32) / head_width)
        * jnp.log(jnp.float32(ROPE_BASE))
    )
    angles = position.astype(jnp.float32)[:, None] * frequency[None, :]
    return (jnp.cos(angles), jnp.sin(angles))


def rotate_fwd(value_tensor, cosine, sine):
    half_width = value_tensor.shape[-1] // 2
    front_half = value_tensor[..., :half_width]
    back_half = value_tensor[..., half_width:]
    return jnp.concatenate(
        [front_half * cosine - back_half * sine, back_half * cosine + front_half * sine], axis=-1
    )


def inverse_rotation(value_tensor, cosine, sine):
    half_width = value_tensor.shape[-1] // 2
    front_half = value_tensor[..., :half_width]
    back_half = value_tensor[..., half_width:]
    return jnp.concatenate(
        [front_half * cosine + back_half * sine, back_half * cosine - front_half * sine], axis=-1
    )


def norm_forward(value_tensor, gain_vector):
    inverse = lax.rsqrt(jnp.mean(value_tensor * value_tensor, axis=-1, keepdims=True) + EPS)
    unit_rows = value_tensor * inverse
    return (unit_rows, inverse, (unit_rows * gain_vector.astype(jnp.float32)).astype(jnp.bfloat16))


def norm_backward(grad_normed, unit_rows, inverse, gain_vector):
    scaled = grad_normed * gain_vector.astype(jnp.float32)
    grad_gain = jnp.sum(grad_normed * unit_rows, axis=0)
    grad_rows = inverse * (
        scaled - unit_rows * jnp.mean(scaled * unit_rows, axis=-1, keepdims=True)
    )
    return (grad_rows, grad_gain)


def block_scores(query_block, key_rows, segment_block, index_block, segment, factor):
    scores = product("qkgd,skd->kgqs", query_block, key_rows) * factor
    length_all = key_rows.shape[0]
    allowed = (segment_block[:, None] == segment[None, :]) & (
        jnp.arange(length_all, dtype=jnp.int32)[None, :] <= index_block[:, None]
    )
    return jnp.where(allowed[None, None], scores, -jnp.inf)


def attend(queries, key_rows, value_row_block, segment, block_rows):
    length_all, kv_heads, query_group_width, head_width = queries.shape
    blocks = length_all // block_rows
    factor = 1.0 / math.sqrt(head_width)
    token_index = jnp.arange(length_all, dtype=jnp.int32)

    def per_block(pieces):
        query_block, segment_block, index_block = pieces
        scores = block_scores(query_block, key_rows, segment_block, index_block, segment, factor)
        maximum = jnp.max(scores, axis=-1, keepdims=True)
        logsum = maximum + jnp.log(jnp.sum(jnp.exp(scores - maximum), axis=-1, keepdims=True))
        weights = jnp.exp(scores - logsum).astype(jnp.bfloat16)
        mixed = product("kgqs,skd->qkgd", weights, value_row_block).astype(jnp.bfloat16)
        return (mixed, logsum[..., 0])

    mixed, logsum = lax.map(
        per_block,
        (
            queries.reshape(blocks, block_rows, kv_heads, query_group_width, head_width),
            segment.reshape(blocks, block_rows),
            token_index.reshape(blocks, block_rows),
        ),
    )
    return (mixed.reshape(length_all, kv_heads, query_group_width, head_width), logsum)


def attend_back(
    queries, key_rows, value_row_block, mixed, mixed_gradient, logsum, segment, block_rows
):
    length_all, kv_heads, query_group_width, head_width = queries.shape
    blocks = length_all // block_rows
    factor = 1.0 / math.sqrt(head_width)
    token_index = jnp.arange(length_all, dtype=jnp.int32)

    def per_block(carry, pieces):
        grad_keys, grad_values = carry
        query_block, mixed_block, grad_block, logsum_block, segment_block, index_block = pieces
        scores = block_scores(query_block, key_rows, segment_block, index_block, segment, factor)
        probability = jnp.exp(scores - logsum_block[..., None])
        grad_values = grad_values + product(
            "kgqs,qkgd->skd", probability.astype(jnp.bfloat16), grad_block
        )
        grad_probs = product("qkgd,skd->kgqs", grad_block, value_row_block)
        row_delta = jnp.sum(
            grad_block.astype(jnp.float32) * mixed_block.astype(jnp.float32), axis=-1
        )
        row_delta = jnp.transpose(row_delta, (1, 2, 0))[..., None]
        grad_scores = (probability * (grad_probs - row_delta) * factor).astype(jnp.bfloat16)
        grad_query = product("kgqs,skd->qkgd", grad_scores, key_rows)
        grad_keys = grad_keys + product("kgqs,qkgd->skd", grad_scores, query_block)
        return ((grad_keys, grad_values), grad_query)

    empty_grad = jnp.zeros((length_all, kv_heads, head_width), jnp.float32)
    shape_blocks = (blocks, block_rows, kv_heads, query_group_width, head_width)
    (grad_keys, grad_values), grad_query = lax.scan(
        per_block,
        (empty_grad, empty_grad),
        (
            queries.reshape(shape_blocks),
            mixed.reshape(shape_blocks),
            mixed_gradient.reshape(shape_blocks),
            logsum,
            segment.reshape(blocks, block_rows),
            token_index.reshape(blocks, block_rows),
        ),
    )
    return (
        grad_query.reshape(length_all, kv_heads, query_group_width, head_width),
        grad_keys,
        grad_values,
    )


def local_plain(
    hidden_in,
    cotangent,
    seq_lengths,
    query_weight,
    key_weight,
    value_weight,
    output_weight,
    w_gate,
    w_up,
    w_down,
    gain_attn,
    gain_mlp,
):
    query_group_width = QUERY_HEADS // KEY_VALUE_HEADS
    gathered = (
        lax.all_gather(query_weight, "dp", axis=0, tiled=True),
        lax.all_gather(key_weight, "dp", axis=0, tiled=True),
        lax.all_gather(value_weight, "dp", axis=0, tiled=True),
        lax.all_gather(output_weight, "dp", axis=1, tiled=True),
        lax.all_gather(w_gate, "dp", axis=0, tiled=True),
        lax.all_gather(w_up, "dp", axis=0, tiled=True),
        lax.all_gather(w_down, "dp", axis=1, tiled=True),
        lax.all_gather(gain_attn, "dp", axis=0, tiled=True),
        lax.all_gather(gain_mlp, "dp", axis=0, tiled=True),
    )
    (
        query_full,
        key_full,
        value_full,
        output_full,
        gate_full,
        up_full,
        down_full,
        gain_one,
        gain_two,
    ) = gathered
    kv_local = key_full.shape[1] // HEAD_SIZE
    unit_one, inverse_one, normed_rows_one = norm_forward(hidden_in, gain_one)
    first_normalized = lax.all_gather(normed_rows_one, "tensor", axis=0, tiled=True)
    tok_rows = first_normalized.shape[0]
    block_rows = min(512, tok_rows)
    segment, position = positions_of(seq_lengths[0], tok_rows)
    cosine, sine = rope_tables(position, HEAD_SIZE)
    cos_heads, sin_heads = (cosine[:, None, None, :], sine[:, None, None, :])
    cosine_key_table, sine_key_table = (cosine[:, None, :], sine[:, None, :])
    unrotated_queries = matrix_multiply(first_normalized, query_full).reshape(
        tok_rows, kv_local, query_group_width, HEAD_SIZE
    )
    unrotated_keys = matrix_multiply(first_normalized, key_full).reshape(
        tok_rows, kv_local, HEAD_SIZE
    )
    value_row_block = (
        matrix_multiply(first_normalized, value_full)
        .astype(jnp.bfloat16)
        .reshape(tok_rows, kv_local, HEAD_SIZE)
    )
    query_rot = rotate_fwd(unrotated_queries, cos_heads, sin_heads).astype(jnp.bfloat16)
    key_rot = rotate_fwd(unrotated_keys, cosine_key_table, sine_key_table).astype(jnp.bfloat16)
    query_rot, key_rot, value_row_block = (query_rot, key_rot, value_row_block)
    mixed, logsum = attend(query_rot, key_rot, value_row_block, segment, block_rows)
    mixed_flat = mixed.reshape(tok_rows, -1)
    residual = hidden_in + lax.psum_scatter(
        matrix_multiply(mixed_flat, output_full), "tensor", scatter_dimension=0, tiled=True
    )
    unit_two, inverse_two, normed_rows_two = norm_forward(residual, gain_two)
    normed_two = lax.all_gather(normed_rows_two, "tensor", axis=0, tiled=True)
    gate_rows = matrix_multiply(normed_two, gate_full)
    up_rows = matrix_multiply(normed_two, up_full)
    sigmoid_gate = jax.nn.sigmoid(gate_rows)
    silu_gate = gate_rows * sigmoid_gate
    project_hidden_act = (silu_gate * up_rows).astype(jnp.bfloat16)
    gate_rows, up_rows, sigmoid_gate, silu_gate, hidden_act = (
        gate_rows,
        up_rows,
        sigmoid_gate,
        silu_gate,
        project_hidden_act,
    )
    block_out = residual + lax.psum_scatter(
        matrix_multiply(hidden_act, down_full).astype(jnp.bfloat16),
        "tensor",
        scatter_dimension=0,
        tiled=True,
    ).astype(jnp.float32)
    gathered = (
        lax.all_gather(query_weight, "dp", axis=0, tiled=True),
        lax.all_gather(key_weight, "dp", axis=0, tiled=True),
        lax.all_gather(value_weight, "dp", axis=0, tiled=True),
        lax.all_gather(output_weight, "dp", axis=1, tiled=True),
        lax.all_gather(w_gate, "dp", axis=0, tiled=True),
        lax.all_gather(w_up, "dp", axis=0, tiled=True),
        lax.all_gather(w_down, "dp", axis=1, tiled=True),
        lax.all_gather(gain_attn, "dp", axis=0, tiled=True),
        lax.all_gather(gain_mlp, "dp", axis=0, tiled=True),
    )
    (
        query_full,
        key_full,
        value_full,
        output_full,
        gate_full,
        up_full,
        down_full,
        gain_one,
        gain_two,
    ) = gathered
    cot_low = lax.all_gather(cotangent.astype(jnp.bfloat16), "tensor", axis=0, tiled=True)
    grad_act = multiply_by_transpose(cot_low, down_full)
    grad_down = transposed_times(hidden_act, cot_low)
    grad_gate_rows = (
        grad_act * up_rows * sigmoid_gate * (1.0 + gate_rows * (1.0 - sigmoid_gate))
    ).astype(jnp.bfloat16)
    grad_up_rows = (grad_act * silu_gate).astype(jnp.bfloat16)
    grad_gate = transposed_times(normed_two, grad_gate_rows)
    grad_upproj = transposed_times(normed_two, grad_up_rows)
    grad_normed_two = lax.psum_scatter(
        (
            multiply_by_transpose(grad_gate_rows, gate_full)
            + multiply_by_transpose(grad_up_rows, up_full)
        ).astype(jnp.bfloat16),
        "tensor",
        scatter_dimension=0,
        tiled=True,
    ).astype(jnp.float32)
    grad_middle, grad_gain_two = norm_backward(grad_normed_two, unit_two, inverse_two, gain_two)
    grad_resid = cotangent + grad_middle
    narrow_gradient = lax.all_gather(grad_resid.astype(jnp.bfloat16), "tensor", axis=0, tiled=True)
    grad_output = transposed_times(mixed_flat, narrow_gradient)
    mixed_gradient = (
        multiply_by_transpose(narrow_gradient, output_full)
        .astype(jnp.bfloat16)
        .reshape(tok_rows, kv_local, query_group_width, HEAD_SIZE)
    )
    grad_qrot, rotated_key_gradient, gradient_values_list = attend_back(
        query_rot, key_rot, value_row_block, mixed, mixed_gradient, logsum, segment, block_rows
    )
    grad_q = (
        inverse_rotation(grad_qrot, cos_heads, sin_heads).astype(jnp.bfloat16).reshape(tok_rows, -1)
    )
    key_gradient = (
        inverse_rotation(rotated_key_gradient, cosine_key_table, sine_key_table)
        .astype(jnp.bfloat16)
        .reshape(tok_rows, -1)
    )
    value_gradient = gradient_values_list.astype(jnp.bfloat16).reshape(tok_rows, -1)
    grad_query = transposed_times(first_normalized, grad_q)
    grad_key = transposed_times(first_normalized, key_gradient)
    grad_value = transposed_times(first_normalized, value_gradient)
    grad_normed_one = lax.psum_scatter(
        (
            multiply_by_transpose(grad_q, query_full)
            + multiply_by_transpose(key_gradient, key_full)
            + multiply_by_transpose(value_gradient, value_full)
        ).astype(jnp.bfloat16),
        "tensor",
        scatter_dimension=0,
        tiled=True,
    ).astype(jnp.float32)
    grad_first, grad_gain_one = norm_backward(grad_normed_one, unit_one, inverse_one, gain_one)
    grad_input = grad_resid + grad_first
    summed = (
        lax.psum_scatter(
            grad_query.astype(jnp.bfloat16), "dp", scatter_dimension=0, tiled=True
        ).astype(jnp.float32),
        lax.psum_scatter(
            grad_key.astype(jnp.bfloat16), "dp", scatter_dimension=0, tiled=True
        ).astype(jnp.float32),
        lax.psum_scatter(
            grad_value.astype(jnp.bfloat16), "dp", scatter_dimension=0, tiled=True
        ).astype(jnp.float32),
        lax.psum_scatter(
            grad_output.astype(jnp.bfloat16), "dp", scatter_dimension=1, tiled=True
        ).astype(jnp.float32),
        lax.psum_scatter(
            grad_gate.astype(jnp.bfloat16), "dp", scatter_dimension=0, tiled=True
        ).astype(jnp.float32),
        lax.psum_scatter(
            grad_upproj.astype(jnp.bfloat16), "dp", scatter_dimension=0, tiled=True
        ).astype(jnp.float32),
        lax.psum_scatter(
            grad_down.astype(jnp.bfloat16), "dp", scatter_dimension=1, tiled=True
        ).astype(jnp.float32),
        lax.psum_scatter(
            grad_gain_one.astype(jnp.bfloat16), "dp", scatter_dimension=0, tiled=True
        ).astype(jnp.float32),
        lax.psum_scatter(
            grad_gain_two.astype(jnp.bfloat16), "dp", scatter_dimension=0, tiled=True
        ).astype(jnp.float32),
    )
    output_grad = summed[3]
    gain_totals = lax.psum((summed[7], summed[8]), "tensor")
    return (
        block_out,
        grad_input,
        summed[0],
        summed[1],
        summed[2],
        output_grad,
        summed[4],
        summed[5],
        summed[6],
        gain_totals[0],
        gain_totals[1],
    )


BF = jnp.bfloat16
F32 = jnp.float32
NEG = -1e30
VMEM_LIMIT = 60 * 1024 * 1024


def dot_nn(a, b):
    return lax.dot_general(a, b, (((1,), (0,)), ((), ())), preferred_element_type=F32)


def dot_nt(a, b):
    return lax.dot_general(a, b, (((1,), (1,)), ((), ())), preferred_element_type=F32)


def dot_tn(a, b):
    return lax.dot_general(a, b, (((0,), (0,)), ((), ())), preferred_element_type=F32)


def whole(shape):
    zeros = (0,) * len(shape)
    return pl.BlockSpec(tuple(shape), lambda *_: zeros)


def call(kernel, name, grid, ins, outs, scalars=(), scratch=(), flops=0):
    moved = sum(a.size * a.dtype.itemsize for a, _ in ins)
    moved += sum(math.prod(s) * jnp.dtype(d).itemsize for s, d, _ in outs)
    return pl.pallas_call(
        kernel,
        name=name,
        out_shape=[jax.ShapeDtypeStruct(s, d) for s, d, _ in outs],
        grid_spec=pltpu.PrefetchScalarGridSpec(
            num_scalar_prefetch=len(scalars),
            grid=grid,
            in_specs=[s for _, s in ins],
            out_specs=[s for _, _, s in outs],
            scratch_shapes=list(scratch),
        ),
        compiler_params=pltpu.CompilerParams(
            dimension_semantics=("arbitrary",) * len(grid), vmem_limit_bytes=VMEM_LIMIT
        ),
        cost_estimate=pl.CostEstimate(flops=int(flops), bytes_accessed=int(moved), transcendentals=0),
    )(*scalars, *[a for a, _ in ins])


def swap_core(x):
    return lax.ppermute(x, "dp", [(i, i ^ 1) for i in range(8)])


def swap_p(x, k):
    return lax.ppermute(x, "dp", [(i, i ^ (2 * k)) for i in range(8)])


def swap_t(x, k):
    return lax.ppermute(x, "tensor", [(i, i ^ k) for i in range(4)])


def shift_up(x):
    return lax.ppermute(x, "tensor", [(i, i + 1) for i in range(3)])


def shift_down(x):
    return lax.ppermute(x, "tensor", [(i + 1, i) for i in range(3)])


def gather_p(x):
    h = x.shape[0] // 2
    one = swap_p(x, 1)
    two = swap_p(x, 2)
    return (x, one, two, swap_p(one[:h], 2), swap_p(two[h:], 1))


def reduce_p(a, b):
    ya = swap_p(a[3], 2)
    xb = swap_p(b[3], 1)
    x1b = swap_p(b[1], 1)
    y2a = swap_p(a[2], 2)
    x1a = swap_p(a[1] + ya, 1)
    y2b = swap_p(b[2] + xb, 2)
    return (
        [(a[0], x1a, y2a), (b[0], x1b, y2b)]
    )


def added(parts, at=None):
    total = None
    for part in parts:
        value = (part if at is None else part[at]).astype(F32)
        total = value if total is None else total + value
    return total


def four(array, rows, width):
    return [
        (array, pl.BlockSpec((rows, width), lambda i, s, r=r: (i, s[0] ^ r))) for r in range(4)
    ]


def cast_kernel(s, a0, a1, a2, a3, out):
    w = a0.shape[1]
    for r, a in enumerate((a0, a1, a2, a3)):
        out[:, r * w : (r + 1) * w] = a[...].astype(BF)


def norm_one_kernel(s, a0, a1, a2, a3, gain, out):
    x = jnp.concatenate([a0[...], a1[...], a2[...], a3[...]], axis=1)
    inv = lax.rsqrt(jnp.mean(x * x, axis=1, keepdims=True) + EPS)
    out[...] = (x * inv * gain[...]).astype(BF)


def norm_two_kernel(s, a0, a1, a2, a3, own, recv, gain, resid, out):
    x = jnp.concatenate([a0[...], a1[...], a2[...], a3[...]], axis=1)
    x = x + own[...] + recv[...].astype(F32)
    resid[...] = x
    inv = lax.rsqrt(jnp.mean(x * x, axis=1, keepdims=True) + EPS)
    out[...] = (x * inv * gain[...]).astype(BF)


def back_two_kernel(s, c0, c1, c2, c3, keep, recv, far, resid, gain, grad, low, gsum):
    cot = jnp.concatenate([c0[...], c1[...], c2[...], c3[...]], axis=1)
    dn = keep[0].astype(F32) + recv[0].astype(F32) + far[...].astype(F32)
    x = resid[...]
    inv = lax.rsqrt(jnp.mean(x * x, axis=1, keepdims=True) + EPS)
    unit = x * inv
    scaled = dn * gain[...]
    value = cot + inv * (scaled - unit * jnp.mean(scaled * unit, axis=1, keepdims=True))
    grad[...] = value
    low[...] = value.astype(BF)

    @pl.when(pl.program_id(0) == 0)
    def _():
        gsum[...] = jnp.zeros_like(gsum)

    gsum[...] += jnp.sum(dn * unit, axis=0, keepdims=True)


def back_one_kernel(s, a0, a1, a2, a3, own, recv, grad, gain, out, gsum):
    x = jnp.concatenate([a0[...], a1[...], a2[...], a3[...]], axis=1)
    dn = own[...] + recv[...].astype(F32)
    inv = lax.rsqrt(jnp.mean(x * x, axis=1, keepdims=True) + EPS)
    unit = x * inv
    scaled = dn * gain[...]
    value = grad[...] + inv * (scaled - unit * jnp.mean(scaled * unit, axis=1, keepdims=True))
    store_natural(s, out, value)

    @pl.when(pl.program_id(0) == 0)
    def _():
        gsum[...] = jnp.zeros_like(gsum)

    gsum[...] += jnp.sum(dn * unit, axis=0, keepdims=True)


def store_natural(s, out, value):
    w = out.shape[1] // 4
    for r in range(4):
        at = pl.multiple_of((s[0] ^ r) * w, 128)
        out[:, pl.ds(at, w)] = value[:, r * w : (r + 1) * w]


def block_out_kernel(s, resid, keep, recv, far, out):
    value = resid[...] + keep[0].astype(F32) + recv[0].astype(F32) + far[...].astype(F32)
    store_natural(s, out, value)


def pack_kernel(s, q, k, v, o, keep_a, send_a, keep_o, send_o):
    def half(ref, h):
        n = ref.shape[1] // 2
        return ref[:, h * n : (h + 1) * n]

    for core in range(2):

        @pl.when(s[0] == core)
        def _(core=core):
            for a_out, o_out, h in ((keep_a, keep_o, core), (send_a, send_o, 1 - core)):
                a_out[...] = jnp.concatenate([half(q, h), half(k, h), half(v, h)], axis=1)
                n = o.shape[0] // 2
                o_out[...] = o[h * n : (h + 1) * n, :]


def rotated(x, cosine, sine):
    n = x.shape[1] // 2
    return x * cosine + jnp.concatenate([x[:, n:], x[:, :n]], axis=1) * sine


def rotated_back(x, cosine, sine):
    n = x.shape[1] // 2
    return x * cosine - jnp.concatenate([x[:, n:], x[:, :n]], axis=1) * sine


def allowed_of(s, lens, b, rows, keys):
    query_at = s[2] + lax.broadcasted_iota(jnp.int32, (rows, 1), 0)
    start = jnp.zeros((rows, 1), jnp.int32)
    end = jnp.int32(0)
    for i in range(lens.shape[1]):
        end = end + lens[b, i]
        start = start + jnp.where(query_at >= end, lens[b, i], 0)
    key_at = s[2] - (keys - rows) + lax.broadcasted_iota(jnp.int32, (rows, keys), 1)
    return (key_at <= query_at) & (key_at >= start)


def pick(j, half, top, bottom):
    return jnp.where(j < half, top, bottom)


def attention_kernel(
    s, lens, x0, x0p, x1, x1p, x2, x2p, w0, w1, w2, w3t, w3b, cos, sin, q_out, k_out, v_out, o_out, l_out
):
    j = pl.program_id(0)
    e = HEAD_SIZE
    w = jnp.concatenate([w0[0], w1[0], w2[0], pick(j, 2, w3t[0], w3b[0])], axis=0)
    factor = 1.0 / math.sqrt(e)
    rows = x0.shape[0]
    keys = 3 * rows
    for b, (own, near, far) in enumerate(((x0, x1, x2), (x0p, x1p, x2p))):
        y = dot_nn(own[...], w)
        halo = jnp.concatenate([far[...], near[...]], axis=0)
        z = dot_nn(halo, w[:, 128:])
        cosine, sine = cos[b], sin[b]
        k = jnp.concatenate([z[:, 2 * e - 128 : 3 * e - 128], y[:, 2 * e : 3 * e]], axis=0)
        k = rotated(k, cosine, sine).astype(BF)
        v = jnp.concatenate([z[:, 3 * e - 128 :], y[:, 3 * e :]], axis=0).astype(BF)
        k_out[0, b] = k
        v_out[0, b] = v
        allowed = allowed_of(s, lens, b, rows, keys)
        mixed = []
        for h in range(2):
            q = rotated(y[:, h * e : (h + 1) * e], cosine[keys - rows :], sine[keys - rows :])
            q = q.astype(BF)
            q_out[0, b, h] = q
            score = jnp.where(allowed, dot_nt(q, k) * factor, NEG)
            top = jnp.max(score, axis=1, keepdims=True)
            weight = jnp.exp(score - top)
            total = jnp.sum(weight, axis=1, keepdims=True)
            l_out[0, b, h] = top + jnp.log(total)
            mixed.append(dot_nn(weight.astype(BF), v) / total)
        o_out[0, b] = jnp.concatenate(mixed, axis=1).astype(BF)


def joined_heads(o):
    return jnp.concatenate([o[j] for j in range(4)], axis=1)


def project_kernel(o, w0, w1, w2, w3t, w3b, own, send):
    rows = o.shape[2]
    n = w0.shape[2]
    ws = [w[...].reshape(-1, n) for w in (w0, w1, w2)]
    ws.append(jnp.concatenate([w3t[...], w3b[...]], axis=0).reshape(-1, n))
    for b, out in ((1, send), (0, own)):
        mixed = jnp.concatenate([o[j, b] for j in range(4)], axis=1)
        for r in range(4):
            out[:, r * n : (r + 1) * n] = dot_nn(mixed, ws[r]).astype(out.dtype)


def attention_back_kernel(
    s, lens, n0, n1, w0, w1, w2, w3, q_in, k_in, v_in, o_in, l_in, cos, sin, d_own, d_near, d_far
):
    e = HEAD_SIZE
    factor = 1.0 / math.sqrt(e)
    rows = n0.shape[0]
    keys = 3 * rows
    w = jnp.concatenate([w0[0], w1[0], w2[0], w3[0]], axis=1)
    for b, low in enumerate((n0, n1)):
        datt = dot_nt(low[...], w).astype(BF)
        product = datt.astype(F32) * o_in[0, b].astype(F32)
        k, v = k_in[0, b], v_in[0, b]
        cosine, sine = cos[b], sin[b]
        allowed = allowed_of(s, lens, b, rows, keys)
        dk = jnp.zeros((keys, e), F32)
        dv = jnp.zeros((keys, e), F32)
        dq = []
        for h in range(2):
            q = q_in[0, b, h]
            da = datt[:, h * e : (h + 1) * e]
            delta = jnp.sum(product[:, h * e : (h + 1) * e], axis=1, keepdims=True)
            score = jnp.where(allowed, dot_nt(q, k) * factor, NEG)
            prob = jnp.exp(score - l_in[0, b, h])
            dscore = (prob * (dot_nt(da, v) - delta) * factor).astype(BF)
            dv = dv + dot_tn(prob.astype(BF), da)
            dk = dk + dot_tn(dscore, q)
            dq.append(rotated_back(dot_nn(dscore, k), cosine[keys - rows :], sine[keys - rows :]))
        dk = rotated_back(dk, cosine, sine)
        own = slice(keys - rows, keys)
        d_own[0, b] = jnp.concatenate([dq[0], dq[1], dk[own], dv[own]], axis=1).astype(BF)
        pad = jnp.zeros((rows, 2 * e - 128), F32)
        for out, at in ((d_far, slice(0, rows)), (d_near, slice(rows, 2 * rows))):
            out[0, b] = jnp.concatenate([pad, dk[at], dv[at]], axis=1).astype(BF)


def attention_grad_kernel(x0, x0p, x1, x1p, x2, x2p, d_own, d_near, d_far, g0, g1, g2, g3, xt):
    m = x0.shape[0]

    @pl.when(pl.program_id(0) == 0)
    def _():
        for i, x in enumerate((x0, x0p, x1, x1p, x2, x2p)):
            xt[:, i * m : (i + 1) * m] = x[...].T

    own = dot_nn(xt[:, : 2 * m], d_own[0].reshape(2 * m, -1))
    halo = jnp.concatenate([d_near[0].reshape(2 * m, -1), d_far[0].reshape(2 * m, -1)], axis=0)
    other = dot_nn(xt[:, 2 * m :], halo)
    total = jnp.concatenate([own[:, :128], own[:, 128:] + other], axis=1).astype(BF)
    n = g0.shape[1]
    for r, g in enumerate((g0, g1, g2, g3)):
        g[0] = total[r * n : (r + 1) * n]


def output_grad_kernel(n0, n1, o, g0a, g0b, g1a, g1b, g2a, g2b, g3a, g3b):
    n = g0a.shape[2]
    low = jnp.concatenate([n0[...], n1[...]], axis=0)
    for j in range(4):
        mixed = o[j].reshape(low.shape[0], -1)
        total = dot_tn(mixed, low).astype(BF)
        outs = (g0a, g1a, g2a, g3a) if j < 2 else (g0b, g1b, g2b, g3b)
        for r, g in enumerate(outs):
            g[j % 2] = total[:, r * n : (r + 1) * n]


def inner_back_kernel(d_own, s_near, w0, w1, w2, w3t, w3b, own, send):
    m = d_own.shape[2]
    ws = [[w[j] for j in range(4)] for w in (w0, w1, w2)]
    ws.append([w3t[0], w3t[1], w3b[0], w3b[1]])
    n = w0.shape[1]
    for b, out in ((1, send), (0, own)):
        ds = []
        for j in range(4):
            d = d_own[j, b]
            extra = d[:, 128:].astype(F32) + s_near[j, b].astype(F32)
            ds += [d[:, :128], extra.astype(BF)]
        d = jnp.concatenate(ds, axis=1)
        for r in range(4):
            out[:, r * n : (r + 1) * n] = dot_nt(d, jnp.concatenate(ws[r], axis=1)).astype(out.dtype)


def hidden_kernel(
    x0, x1, x2, x3, c0, c1, c2, c3, a0, a1, a2, a3t, a3b, d0, d1, d2, d3t, d3b, z_out
):
    q = pl.program_id(0)
    x = jnp.concatenate([x0[...], x1[...], x2[...], x3[...]], axis=0)
    cot = jnp.concatenate([c0[...], c1[...], c2[...], c3[...]], axis=0)

    def weight(i):
        return jnp.concatenate([a0[i], a1[i], a2[i], pick(q, 1, a3t[i], a3b[i])], axis=0)

    gate = dot_nn(x, weight(0))
    up = dot_nn(x, weight(1))
    down = jnp.concatenate([d0[0], d1[0], d2[0], pick(q, 1, d3t[0], d3b[0])], axis=0)
    dact = dot_nn(cot, down)
    sig = 1.0 / (1.0 + jnp.exp(-gate))
    silu = gate * sig
    z_out[0, 0] = (dact * up * sig * (1.0 + gate * (1.0 - sig))).astype(BF)
    z_out[1, 0] = (dact * silu).astype(BF)
    z_out[2, 0] = (silu * up).astype(BF)


def hidden_back_kernel(count, z, w0, w1, w2, w3t, w3b, send, keep):
    i = pl.program_id(0)
    n = w0.shape[1]
    lhs, ws = [], [[], [], [], []]
    for q in range(2):
        for m in range(count):
            lhs.append(z[m, q])
            for r, w in enumerate((w0, w1, w2)):
                ws[r].append(w[q * count + m])
            ws[3].append((w3t, w3b)[q][m])
    lhs = jnp.concatenate(lhs, axis=1)
    parts = [dot_nt(lhs, jnp.concatenate(w, axis=1)).astype(BF) for w in ws]

    @pl.when(i < 2)
    def _():
        for r in range(4):
            send[0, :, r * n : (r + 1) * n] = parts[r]

    @pl.when(i >= 2)
    def _():
        for r in range(4):
            keep[0, :, r * n : (r + 1) * n] = parts[r]


def hidden_grad_kernel(x0, x1, x2, x3, c0, c1, c2, c3, z, g0, g1, g2, g3, xt):
    m = pl.program_id(0)
    rows = x0.shape[0]

    @pl.when(m == 0)
    def _():
        for i, x in enumerate((x0, x1, x2, x3)):
            xt[:, i * rows : (i + 1) * rows] = x[...].T

    @pl.when(m == 2)
    def _():
        for i, x in enumerate((c0, c1, c2, c3)):
            xt[:, i * rows : (i + 1) * rows] = x[...].T

    total = dot_nn(xt[...], z[0, 0]).astype(BF)
    n = g0.shape[1]
    for r, g in enumerate((g0, g1, g2, g3)):
        g[0] = total[r * n : (r + 1) * n]


def local_fast(
    hidden_in,
    cotangent,
    seq_lengths,
    query_weight,
    key_weight,
    value_weight,
    output_weight,
    w_gate,
    w_up,
    w_down,
    gain_attn,
    gain_mlp,
):
    plane = lax.axis_index("dp") // 2
    core = lax.axis_index("dp") % 2
    level = lax.axis_index("tensor")
    first = core == 0
    rows, width = hidden_in.shape
    quarter = width // 4
    shard = quarter // 2
    sp = jnp.stack([plane, core, level * rows]).astype(jnp.int32)
    sc = sp[1:2]

    def merged(mine, theirs, axis):
        return jnp.where(
            first,
            jnp.concatenate([mine, theirs], axis=axis),
            jnp.concatenate([theirs, mine], axis=axis),
        )

    gains = jnp.stack([gain_attn, gain_mlp]).astype(F32)
    gains = merged(gains, swap_core(gains), 1)
    gains = jnp.concatenate([gains, swap_p(gains, 1), swap_p(gains, 2), swap_p(gains, 3)], axis=1)
    gain_one, gain_two = gains[0:1], gains[1:2]
    lens = jnp.concatenate([seq_lengths, swap_core(seq_lengths)], axis=0)

    qkv = (query_weight.shape[1] + key_weight.shape[1] + value_weight.shape[1]) // 2
    wide_o = output_weight.shape[0] // 2
    keep_a, send_a, keep_o, send_o = call(
        pack_kernel,
        "pack",
        (1,),
        [(w, whole(w.shape)) for w in (query_weight, key_weight, value_weight, output_weight)],
        [
            ((shard, qkv), BF, whole((shard, qkv))),
            ((shard, qkv), BF, whole((shard, qkv))),
            ((wide_o, shard), BF, whole((wide_o, shard))),
            ((wide_o, shard), BF, whole((wide_o, shard))),
        ],
        scalars=(sc,),
    )
    a_own = merged(keep_a, swap_core(send_a), 0)
    a_all = jnp.stack([a_own, swap_t(a_own, 1), swap_t(a_own, 2), swap_t(a_own, 3)])
    a_pieces = gather_p(a_all)
    o_own = merged(keep_o, swap_core(send_o), 1)
    o_all = jnp.stack([o_own, swap_t(o_own, 1), swap_t(o_own, 2), swap_t(o_own, 3)])
    o_pieces = gather_p(o_all)

    ff = w_gate.shape[1] // 2
    trio = jnp.stack([w_gate, w_up, w_down.T])
    mine = jnp.where(first, trio[:, :, :ff], trio[:, :, ff:])
    other = jnp.where(first, trio[:, :, ff:], trio[:, :, :ff])
    trio = merged(mine, swap_core(other), 1)
    far_trio = swap_t(trio, 2)
    gu_all = jnp.concatenate([trio[:2], far_trio[:2]], axis=0)
    d_all = jnp.concatenate([trio[2:], far_trio[2:]], axis=0)
    gu_pieces = gather_p(gu_all)
    d_pieces = gather_p(d_all)

    tile = rows // 4
    row_full = pl.BlockSpec((tile, width), lambda i, s: (i, 0))
    gain_spec = pl.BlockSpec((1, width), lambda i, s: (0, 0))
    (n_one,) = call(
        norm_one_kernel,
        "norm_one",
        (4,),
        four(hidden_in, tile, quarter) + [(gain_one, gain_spec)],
        [((rows, width), BF, row_full)],
        scalars=(sp,),
    )
    (cot,) = call(
        cast_kernel, "cot", (4,), four(cotangent, tile, quarter), [((rows, width), BF, row_full)], scalars=(sp,)
    )
    near = shift_up(n_one)
    far = shift_up(near)
    xs = (n_one, swap_core(n_one), near, swap_core(near), far, swap_core(far))

    token = jnp.arange(3 * rows, dtype=jnp.int32) + level * rows - 2 * rows
    ends = jnp.cumsum(lens, axis=1)
    starts = jnp.sum(
        jnp.where(token[None, :, None] >= ends[:, None, :], lens[:, None, :], 0), axis=2
    )
    cosine, sine = rope_tables((token[None, :] - starts).reshape(-1), HEAD_SIZE)
    cosine = jnp.concatenate([cosine, cosine], axis=1).reshape(2, 3 * rows, HEAD_SIZE)
    sine = jnp.concatenate([-sine, sine], axis=1).reshape(2, 3 * rows, HEAD_SIZE)

    def per_j(shape, offset=0):
        tail = (0,) * (len(shape) - 1)
        return pl.BlockSpec((1,) + tuple(shape[1:]), lambda j, *_: (j + offset,) + tail)

    def top_j(shape):
        tail = (0,) * (len(shape) - 1)
        return pl.BlockSpec((1,) + tuple(shape[1:]), lambda j, *_: (jnp.minimum(j, 1),) + tail)

    def bottom_j(shape):
        tail = (0,) * (len(shape) - 1)
        return pl.BlockSpec((1,) + tuple(shape[1:]), lambda j, *_: (jnp.maximum(j - 2, 0),) + tail)

    def piece_specs(pieces):
        kinds = (per_j, per_j, per_j, top_j, bottom_j)
        return [(x, kind(x.shape)) for x, kind in zip(pieces, kinds)]

    e = HEAD_SIZE
    q_shape, k_shape = (4, 2, 2, rows, e), (4, 2, 3 * rows, e)
    o_shape, l_shape = (4, 2, rows, 2 * e), (4, 2, 2, rows, 1)
    q_rot, k_rot, v_all, mixed, lse = call(
        attention_kernel,
        "attention",
        (4,),
        [(x, whole(x.shape)) for x in xs]
        + piece_specs(a_pieces)
        + [(cosine, whole(cosine.shape)), (sine, whole(sine.shape))],
        [
            (q_shape, BF, per_j(q_shape)),
            (k_shape, BF, per_j(k_shape)),
            (k_shape, BF, per_j(k_shape)),
            (o_shape, BF, per_j(o_shape)),
            (l_shape, F32, per_j(l_shape)),
        ],
        scalars=(sp, lens),
        flops=12e9,
    )
    flat = (rows, width)
    own, send = call(
        project_kernel,
        "project",
        (1,),
        [(mixed, whole(mixed.shape))] + [(w, whole(w.shape)) for w in o_pieces],
        [(flat, F32, whole(flat)), (flat, BF, whole(flat))],
        flops=1.3e9,
    )
    recv = swap_core(send)
    resid, n_two = call(
        norm_two_kernel,
        "norm_two",
        (4,),
        four(hidden_in, tile, quarter) + [(own, row_full), (recv, row_full), (gain_two, gain_spec)],
        [(flat, F32, row_full), (flat, BF, row_full)],
        scalars=(sp,),
    )

    n_far = swap_t(n_two, 1)
    hs = (swap_core(n_far), swap_core(n_two), n_far, n_two)
    cot_far = swap_t(cot, 1)
    cots = (swap_core(cot_far), swap_core(cot), cot_far, cot)
    half = ff // 2

    def unit_specs(pieces, count):
        out = []
        for i, x in enumerate(pieces):
            if i < 3:
                spec = pl.BlockSpec((count, quarter, half), lambda q, h: (q, 0, h))
            else:
                spec = pl.BlockSpec((count, quarter, half), lambda q, h: (0, 0, h))
            out.append((x, spec))
        return out

    tokens = 4 * rows
    z_shape = (3, 2, tokens, ff)
    (z,) = call(
        hidden_kernel,
        "hidden",
        (2, 2),
        [(x, whole(x.shape)) for x in hs + cots] + unit_specs(gu_pieces, 2) + unit_specs(d_pieces, 1),
        [(z_shape, BF, pl.BlockSpec((3, 1, tokens, half), lambda q, h: (0, q, 0, h)))],
        flops=9.7e9,
    )
    two = (2, rows, width)
    send_spec = pl.BlockSpec((1, rows, width), lambda i: (jnp.minimum(i, 1), 0, 0))
    keep_spec = pl.BlockSpec((1, rows, width), lambda i: (jnp.maximum(i - 2, 0), 0, 0))

    def hidden_back(name, at, count, pieces):
        return call(
            lambda *refs: hidden_back_kernel(count, *refs),
            name,
            (4,),
            [(z, pl.BlockSpec((count, 2, rows, ff), lambda i: (at, 0, i, 0)))]
            + [(w, whole(w.shape)) for w in pieces],
            [(two, BF, send_spec), (two, BF, keep_spec)],
            flops=count * 3.2e9,
        )

    def to_owner(send, keep):
        recv = swap_core(send)
        pair = (keep[0].astype(F32) + recv[0].astype(F32)).astype(BF)
        return keep, recv, swap_t(pair, 1)

    g_send, g_keep = hidden_back("hidden_back", 0, 2, gu_pieces)
    g_keep, g_recv, g_far = to_owner(g_send, g_keep)

    def second(shape):
        return pl.BlockSpec((1, tile, width), lambda i, s: (1, i, 0))

    grad_resid, low, gsum_two = call(
        back_two_kernel,
        "back_two",
        (4,),
        four(cotangent, tile, quarter)
        + [(g_keep, second(two)), (g_recv, second(two)), (g_far, row_full), (resid, row_full), (gain_two, gain_spec)],
        [(flat, F32, row_full), (flat, BF, row_full), ((1, width), F32, gain_spec)],
        scalars=(sp,),
    )
    lows = (low, swap_core(low))

    g_shape = (3, quarter, ff)

    def hidden_grad(q):
        return call(
            hidden_grad_kernel,
            "hidden_grad",
            (3,),
            [(x, whole(x.shape)) for x in hs + cots]
            + [(z, pl.BlockSpec((1, 1, tokens, ff), lambda m: (m, q, 0, 0)))],
            [(g_shape, BF, pl.BlockSpec((1, quarter, ff), lambda m: (m, 0, 0)))] * 4,
            scratch=[pltpu.VMEM((width, tokens), BF)],
            flops=4.8e9,
        )

    grads_b = hidden_grad(1)
    grads_a = hidden_grad(0)
    sum_a, sum_b = reduce_p(grads_a, grads_b)
    f_far = swap_t(added(sum_b).astype(BF), 2)
    f_total = added(sum_a) + f_far.astype(F32)

    b_send, b_keep = hidden_back("hidden_out", 2, 1, d_pieces)
    b_keep, b_recv, b_far = to_owner(b_send, b_keep)
    (block_out,) = call(
        block_out_kernel,
        "block_out",
        (4,),
        [(resid, row_full), (b_keep, second(two)), (b_recv, second(two)), (b_far, row_full)],
        [(flat, F32, row_full)],
        scalars=(sp,),
    )

    og_half = (2, wide_o, quarter)
    og = call(
        output_grad_kernel,
        "output_grad",
        (1,),
        [(x, whole(x.shape)) for x in lows + (mixed,)],
        [(og_half, BF, whole(og_half))] * 8,
        flops=1.3e9,
    )
    o_sum_a, o_sum_b = reduce_p(og[0::2], og[1::2])

    d_shape, n_shape = (2, 2, rows, 4 * e), (2, 2, rows, 256)
    ga_half = (2, quarter, qkv)

    def attention_back(j0, third):
        def at(x):
            return (x, per_j(x.shape, j0))

        return call(
            attention_back_kernel,
            "attention_back",
            (2,),
            [(x, whole(x.shape)) for x in lows]
            + [at(x) for x in o_pieces[:3]]
            + [(third, per_j(third.shape))]
            + [at(x) for x in (q_rot, k_rot, v_all, mixed, lse)]
            + [(cosine, whole(cosine.shape)), (sine, whole(sine.shape))],
            [
                (d_shape, BF, per_j(d_shape)),
                (n_shape, BF, per_j(n_shape)),
                (n_shape, BF, per_j(n_shape)),
            ],
            scalars=(sp, lens),
            flops=4e9,
        )

    def attention_grad(ds):
        return call(
            attention_grad_kernel,
            "attention_grad",
            (2,),
            [(x, whole(x.shape)) for x in xs] + [(d, per_j(d.shape)) for d in ds],
            [(ga_half, BF, per_j(ga_half))] * 4,
            scratch=[pltpu.VMEM((width, 6 * rows), BF)],
            flops=5e9,
        )

    ds_b = attention_back(2, o_pieces[4])
    ag_b = attention_grad(ds_b)
    ds_a = attention_back(0, o_pieces[3])
    ag_a = attention_grad(ds_a)
    a_sum_a, a_sum_b = reduce_p(ag_a, ag_b)

    d_own, d_near, d_far = (jnp.concatenate([a, b], axis=0) for a, b in zip(ds_a, ds_b))
    even = level % 2 == 0

    def refit(x):
        pairs = jnp.concatenate([x[1:2], x[0:1], x[3:4], x[2:3]], axis=0)
        back = jnp.concatenate([x[3:4], x[2:3], x[1:2], x[0:1]], axis=0)
        return jnp.where(even, pairs, back)

    s_near = (d_near.astype(F32) + refit(shift_down(d_far)).astype(F32)).astype(BF)
    s_near = refit(shift_down(s_near))
    own, send = call(
        inner_back_kernel,
        "inner_back",
        (1,),
        [(x, whole(x.shape)) for x in (d_own, s_near) + tuple(a_pieces)],
        [(flat, F32, whole(flat)), (flat, BF, whole(flat))],
        flops=2.5e9,
    )
    recv = swap_core(send)
    grad_input, gsum_one = call(
        back_one_kernel,
        "back_one",
        (4,),
        four(hidden_in, tile, quarter)
        + [(own, row_full), (recv, row_full), (grad_resid, row_full), (gain_one, gain_spec)],
        [(flat, F32, row_full), ((1, width), F32, gain_spec)],
        scalars=(sp,),
    )

    def over_levels(sum_a, sum_b):
        to = [added(sum_a, 1), added(sum_b, 0), added(sum_b, 1)]
        total = added(sum_a, 0)
        for k in range(3):
            total = total + swap_t(to[k].astype(BF), k + 1).astype(F32)
        return total

    a_total = over_levels(a_sum_a, a_sum_b)
    o_total = over_levels(o_sum_a, o_sum_b)

    def split(total, axis):
        n = total.shape[axis] // 2
        low_part = lax.slice_in_dim(total, 0, n, axis=axis)
        high_part = lax.slice_in_dim(total, n, 2 * n, axis=axis)
        mine = jnp.where(first, low_part, high_part)
        theirs = swap_core(jnp.where(first, high_part, low_part).astype(BF)).astype(F32)
        return mine, theirs

    mine, theirs = split(a_total, 0)
    cuts = (0, 2 * e, 3 * e, 4 * e)
    grad_query, grad_key, grad_value = (
        merged(mine[:, i:k], theirs[:, i:k], 1) for i, k in zip(cuts[:-1], cuts[1:])
    )
    mine, theirs = split(o_total, 1)
    grad_output = merged(mine, theirs, 0)
    mine, theirs = split(f_total, 1)
    f_grads = merged(mine, theirs, 2)

    gsums = jnp.concatenate([gsum_one, gsum_two], axis=0)
    gsums = gsums + swap_core(gsums)
    gsums = gsums + swap_t(gsums, 1)
    gsums = gsums + swap_t(gsums, 2)
    total = gsums[:, :quarter]
    for k in range(1, 4):
        total = total + swap_p(gsums[:, k * quarter : (k + 1) * quarter], k)
    total = jnp.where(first, total[:, :shard], total[:, shard:])
    return (
        block_out,
        grad_input,
        grad_query,
        grad_key,
        grad_value,
        grad_output,
        f_grads[0],
        f_grads[1],
        f_grads[2].T,
        total[0],
        total[1],
    )


def solution(mesh):
    wide = mesh.shape["dp"] == 8 and mesh.shape["tensor"] == 4
    body = local_fast if wide else local_plain
    in_specs = (
        P(("dp", "tensor"), None),
        P(("dp", "tensor"), None),
        P("dp", None),
        P("dp", "tensor"),
        P("dp", "tensor"),
        P("dp", "tensor"),
        P("tensor", "dp"),
        P("dp", "tensor"),
        P("dp", "tensor"),
        P("tensor", "dp"),
        P("dp"),
        P("dp"),
    )
    out_specs = (
        P(("dp", "tensor"), None),
        P(("dp", "tensor"), None),
        P("dp", "tensor"),
        P("dp", "tensor"),
        P("dp", "tensor"),
        P("tensor", "dp"),
        P("dp", "tensor"),
        P("dp", "tensor"),
        P("tensor", "dp"),
        P("dp"),
        P("dp"),
    )
    return jax.shard_map(body, mesh=mesh, in_specs=in_specs, out_specs=out_specs, check_vma=False)
```
